32 devices in a mesh: groups: 2 (over y), row: 4 (over z), col: 4 (over x, core).
Axes of the slice: x: 2, y: 2, z: 4, core: 2. Of those that a mesh axis runs over, the one named last changes fastest.
Arguments:
- left_act: float32 [256, 32, 32], P(('groups', 'row'), 'col'), parts along dimension 0, may hold values from -6 to 6
- right_act: float32 [256, 32, 32], P(('groups', 'row'), 'col'), parts along dimension 0, may hold values from -6 to 6
- weight: float32 [1024, 128], replicated, may hold values from -0.75 to 0.75
- bias: float32 [128], replicated, may hold values from -1.8 to 1.8
- cotangent: float32 [64, 32, 128], P(('groups', 'row'), 'col'), parts along dimension 0, may hold values from -0.6 to 0.6
Outputs:
- pair: float32 [64, 32, 128], P(('groups', 'row'), 'col'), parts along dimension 0
- grad_left: float32 [256, 32, 32], P(('groups', 'row'), 'col'), parts along dimension 0
- grad_right: float32 [256, 32, 32], P(('groups', 'row'), 'col'), parts along dimension 0
- grad_weight: float32 [2048, 128], P(('groups', 'row')), parts along dimension 0
The draws below stay inside these ranges and needn't reach their ends.
There are 2 independent parts, one for each index of `groups`. The reference program is written for one: setup_inputs(seed, part) draws one part's arguments, and reference() takes and returns one part's arrays. A program takes and returns all parts, laid end to end along the dimension named above; an argument that names none is the same for every part. Nothing has to cross between parts.
All inputs are finite; a program needn't handle non-finite values.
Results may differ from the reference program's by a relative error of at most 0.0003.
Values sent between devices are 32-bit elements; how exact they have to be, the bound alone decides.
A program may use at most 64 MiB of HBM per device.

```python
import math
import jax
import jax.numpy as jnp
from jax import lax

C = 32
Z = 128
S = 128
R = 32


def block_scale(stream_key, extent, pieces, least, high):
    loudness = 1.0
    for position, blocks in pieces:
        steps = jax.random.uniform(jax.random.fold_in(jax.random.fold_in(stream_key, 6), position), (blocks,), jnp.float32, least / len(pieces), high / len(pieces))
        loudness = loudness * jnp.repeat(jnp.exp(steps), extent[position] // blocks).reshape((-1,) + (1,) * (len(extent) - 1 - position))
    return loudness


def centred(rng, extent, scale, bound, shards=(), kind=jnp.bfloat16):
    values = scale * jax.random.normal(rng, extent, jnp.float32)
    if shards:
        values = values * block_scale(rng, extent, shards, -0.22, 0.18)
    return jnp.clip(values, -bound, bound).astype(kind)


def setup_inputs(seed: int = 0, part: int = 0) -> dict:
    keys = jax.random.split(jax.random.key(seed), 6)
    part_splits = jax.random.split(jax.random.fold_in(keys[5], part), 6)
    left_act = centred(part_splits[0], (S, R, C), 1.0, 6.0, ((0, 4), (1, 4)), jnp.float32)
    right_act = centred(part_splits[1], (S, R, C), 1.0, 6.0, ((0, 4), (1, 4)), jnp.float32)
    weight = centred(keys[2], (C * C, Z), (C * C // 16) ** -0.5, 0.75, (), jnp.float32)
    bias = centred(keys[3], (Z,), 0.3, 1.8, (), jnp.float32)
    cotangent = centred(part_splits[4], (R, R, Z), 0.1, 0.6, ((0, 4), (1, 4)), jnp.float32)
    return {"left_act": left_act, "right_act": right_act, "weight": weight, "bias": bias, "cotangent": cotangent}


def block_terms(left_block, right_full, cot_block, weight_cube, bias):
    seqs = right_full.shape[0]
    highest = lax.Precision.HIGHEST
    products = jnp.einsum("sic,sjd->icjd", left_block, right_full, precision=highest) / seqs
    pair_block = jnp.einsum("icjd,cdz->ijz", products, weight_cube, precision=highest) + bias
    grad_outer = jnp.einsum("ijz,cdz->icjd", cot_block, weight_cube, precision=highest)
    weight_term = jnp.einsum("icjd,ijz->cdz", products, cot_block, precision=highest)
    left_term = jnp.einsum("icjd,sjd->sic", grad_outer, right_full, precision=highest) / seqs
    right_term = jnp.einsum("icjd,sic->sjd", grad_outer, left_block, precision=highest) / seqs
    return pair_block, weight_term, left_term, right_term


def reference(left_act, right_act, weight, bias, cotangent):
    residues = left_act.shape[1]
    width = left_act.shape[2]
    pair_width = weight.shape[1]
    block_rows = math.gcd(residues, 32)
    block_count = residues // block_rows
    weight_cube = weight.reshape(width, width, pair_width)

    def one_block(totals, block_index):
        start = (block_index * block_rows).astype(jnp.int32)
        left_block = lax.dynamic_slice_in_dim(left_act, start, block_rows, 1)
        cot_block = lax.dynamic_slice_in_dim(cotangent, start, block_rows, 0)
        pair_block, weight_term, left_term, right_term = block_terms(left_block, right_act, cot_block, weight_cube, bias)
        return (totals[0] + weight_term, totals[1] + right_term), (pair_block, left_term)

    initial = (jnp.zeros((width, width, pair_width), jnp.float32), jnp.zeros(right_act.shape, jnp.float32))
    (grad_cube, grad_right), (pair_blocks, left_blocks) = lax.scan(one_block, initial, jnp.arange(block_count, dtype=jnp.int32))
    pair = pair_blocks.reshape(residues, residues, pair_width)
    grad_left = jnp.transpose(left_blocks, (1, 0, 2, 3)).reshape(left_act.shape)
    return pair, grad_left, grad_right, grad_cube.reshape(width * width, pair_width)
```

```python
import functools

import jax
import jax.numpy as jnp
from jax import lax
from jax.experimental import pallas as pl
from jax.experimental.pallas import tpu as pltpu
from jax.sharding import PartitionSpec as P

LANES = 128
SUBLANES = 8
NN = (((1,), (0,)), ((), ()))
NT = (((1,), (1,)), ((), ()))


def split(value):
    high = value.astype(jnp.bfloat16)
    low = (value - high.astype(jnp.float32)).astype(jnp.bfloat16)
    return high, low


def product(a, b, dims):
    dot = functools.partial(lax.dot_general, dimension_numbers=dims, preferred_element_type=jnp.float32)
    return dot(a[0], b[1]) + dot(a[1], b[0]) + dot(a[0], b[0])


def swap_groups(tiles, width):
    lane = lax.broadcasted_iota(jnp.int32, tiles[0].shape, 1)
    low_half = lane < 2 * width
    even = lax.rem(lane // width, 2) == 0
    x = list(tiles)
    for p in (0, 1):
        a, b = x[p], x[p + 2]
        x[p] = jnp.where(low_half, a, pltpu.roll(b, 2 * width, 1))
        x[p + 2] = jnp.where(low_half, pltpu.roll(a, 2 * width, 1), b)
    for p in (0, 2):
        a, b = x[p], x[p + 1]
        x[p] = jnp.where(even, a, pltpu.roll(b, width, 1))
        x[p + 1] = jnp.where(even, pltpu.roll(a, LANES - width, 1), b)
    return x


def fused_kernel(
    n, seqs, left_count, right_count, width, pair_width,
    l_hbm, r_hbm, w_hbm, b_hbm, c_hbm,
    pair_ref, gl_ref, gr_ref, gw_ref,
    lv, rv, wv, bv, lpack, rpack, lsend, lrecv, lmt, lmid, ltbuf, lrow, rbuf, cotbuf,
    whi, wlo, outer2, pairs, pairb, gop, gls, glb, gws, gwa, gwx, gwf, gwo,
    in_sem, ls_sem, lr_sem, rs_sem, rr_sem, cs_sem, cr_sem, rows_sem, rowr_sem,
    ms_sem, mr_sem, ps_sem, pr_sem, gls_sem, glr_sem, as_sem, ar_sem,
):
    group, row, col = lax.axis_index("groups"), lax.axis_index("row"), lax.axis_index("col")
    share = seqs // n
    quads = LANES // width
    block = width // n
    left_all = n * left_count
    halves = right_count // quads
    lanes_r = right_count * width
    core = lax.rem(col, 2)
    mate = col + 1 - 2 * core
    across = lax.rem(col + 2, n)
    others = (2, 1, 3)

    def remote(src, dst, send, recv, to_row, to_col):
        return pltpu.make_async_remote_copy(
            src_ref=src, dst_ref=dst, send_sem=send, recv_sem=recv,
            device_id=(group, to_row, to_col), device_id_type=pl.DeviceIdType.MESH,
        )

    def rows_of(k):
        return lax.rem(row + k, n)

    def cols_of(k):
        return lax.rem(col + k, n)

    barrier = pltpu.get_barrier_semaphore()
    for k in others:
        for to in ((rows_of(k), col), (row, cols_of(k))):
            pl.semaphore_signal(
                barrier, inc=1, device_id=(group,) + to, device_id_type=pl.DeviceIdType.MESH,
            )
    own_rows = pl.ds(pl.multiple_of(row * left_count, left_count), left_count)
    own_cols = pl.ds(pl.multiple_of(col * left_count, left_count), left_count)
    loads = [
        pltpu.make_async_copy(src, dst, in_sem.at[at])
        for at, (src, dst) in enumerate(
            ((l_hbm, lv), (r_hbm, rv), (w_hbm, wv), (b_hbm, bv), (c_hbm, cotbuf.at[own_rows]))
        )
    ]
    for load in loads:
        load.start()

    loads[0].wait()
    for i in range(left_count):
        lpack[:, i * width:(i + 1) * width] = lv[pl.ds(i, share, stride=left_count), :]
    loads[1].wait()
    for j in range(right_count):
        rpack[:, j * width:(j + 1) * width] = rv[pl.ds(j, share, stride=right_count), :]
    left_t = lpack[...].T
    for q in range(n):
        for i in range(left_count):
            hi, lo = i // quads, i % quads
            lsend[q, hi * block:(hi + 1) * block, lo * share:(lo + 1) * share] = (
                left_t[i * width + q * block:i * width + (q + 1) * block, :]
            )
    pl.semaphore_wait(barrier, 2 * (n - 1))

    sends = []

    def send(*args):
        copy = remote(*args)
        copy.start()
        sends.append(copy)

    for k in others:
        to = rows_of(k)
        send(lsend.at[to], lrecv.at[row], ls_sem.at[k - 1], lr_sem.at[row], to, col)
    for k in others:
        send(rpack, rbuf.at[row], rs_sem.at[k - 1], rr_sem.at[row], rows_of(k), col)
    for k in others:
        send(lpack, lrow.at[col], rows_sem.at[k - 1], rowr_sem.at[col], row, cols_of(k))
    for k in others:
        send(c_hbm, cotbuf.at[own_rows], cs_sem.at[k - 1], cr_sem.at[row], rows_of(k), col)
    lrecv[row] = lsend[row]
    rbuf[row] = rpack[...]
    lrow[col] = lpack[...]

    loads[2].wait()
    high, low = split(wv[...])
    whi[...] = high
    wlo[...] = low

    for k in range(1, n):
        at = rows_of(k)
        pltpu.make_async_copy(lsend.at[0], lrecv.at[at], lr_sem.at[at]).wait()
    for hi in range(left_count // quads):
        tiles = [lrecv[k, hi * block:(hi + 1) * block, :] for k in range(n)]
        for lo, tile in enumerate(swap_groups(tiles, width)):
            at = (hi * quads + lo) * block
            lmt[at:at + block, :] = tile
    for c in range(block):
        lmid[c] = lmt[pl.ds(c, left_count, stride=block), :]
    for k in others:
        send(lmid, ltbuf.at[:, own_cols], ms_sem.at[k - 1], mr_sem.at[col], row, cols_of(k))
    ltbuf[:, own_cols, :] = lmid[...]

    for k in range(1, n):
        at = rows_of(k)
        pltpu.make_async_copy(rpack, rbuf.at[at], rr_sem.at[at]).wait()
    right_parts = split(rbuf[...].reshape(seqs, lanes_r))
    for k in range(1, n):
        at = cols_of(k)
        pltpu.make_async_copy(lmid, lmid, mr_sem.at[at]).wait()
    left_parts = split(ltbuf[...].reshape(block * left_all, seqs))
    outer = product(left_parts, right_parts, NN) * (1.0 / seqs)
    for m in range(n):
        for h in range(halves):
            for q in range(block // quads):
                tiles = []
                for a in range(quads):
                    at = ((q * quads + a) * n + m) * left_count
                    tiles.append(outer[at:at + left_count, h * LANES:(h + 1) * LANES])
                for b, tile in enumerate(swap_groups(tiles, width)):
                    at = ((h * quads + b) * n + m) * left_count
                    outer2[at:at + left_count, q * LANES:(q + 1) * LANES] = tile
    w_rows = pl.ds(pl.multiple_of(row * block * width, block * width), block * width)
    outer_parts = split(outer2[...])
    pairs[...] = product(outer_parts, (whi[w_rows, :], wlo[w_rows, :]), NN).reshape(pairs.shape)
    for k in others:
        to = rows_of(k)
        piece = pl.ds(pl.multiple_of(to * left_count, left_count), left_count)
        send(pairs.at[:, piece], pairb.at[row], ps_sem.at[k - 1], pr_sem.at[row], to, col)
    outer_t = split(outer2[...].T)

    loads[4].wait()
    for k in range(1, n):
        at = rows_of(k)
        pltpu.make_async_copy(c_hbm, cotbuf.at[own_rows], cr_sem.at[at]).wait()
    cot = jnp.concatenate(
        [cotbuf[:, j, :] for j in range(right_count)], axis=0
    )
    cot_parts = split(cot)
    gws[...] = product(outer_t, cot_parts, NN).reshape(gws.shape)
    first = remote(gws.at[1 - core], gwa, as_sem.at[0], ar_sem.at[0], row, mate)
    first.start()

    go2 = product(cot_parts, (whi[...], wlo[...]), NT) * (1.0 / seqs)
    for m in range(n):
        for h in range(halves):
            for q in range(width // quads):
                tiles = []
                for b in range(quads):
                    at = ((h * quads + b) * n + m) * left_count
                    tiles.append(go2[at:at + left_count, q * LANES:(q + 1) * LANES])
                for a, tile in enumerate(swap_groups(tiles, width)):
                    at = (m * width + q * quads + a) * left_count
                    gop[h, at:at + left_count, :] = tile

    first.wait_recv()
    gwx_own = gws[core] + gwa[...]
    gwf[...] = gwx_own
    second = remote(gwf, gwx, as_sem.at[1], ar_sem.at[1], row, across)
    second.start()

    grad_outer = jnp.concatenate(
        [
            jnp.concatenate(
                [
                    gop[h, pl.ds(m * width * left_count + i, width, stride=left_count), :]
                    for m in range(n) for i in range(left_count)
                ],
                axis=0,
            )
            for h in range(halves)
        ],
        axis=1,
    )
    go_parts = split(grad_outer)
    own_parts = split(rpack[...])
    gl_part = product(own_parts, go_parts, NT)
    for m in range(n):
        gls[m] = gl_part[:, m * left_count * width:(m + 1) * left_count * width]
    for k in others:
        to = cols_of(k)
        send(gls.at[to], glb.at[col], gls_sem.at[k - 1], glr_sem.at[col], row, to)

    for k in range(1, n):
        at = cols_of(k)
        pltpu.make_async_copy(lpack, lrow.at[at], rowr_sem.at[at]).wait()
    gr = None
    for m in range(n):
        lanes = left_count * width
        part = product(
            split(lrow[m]), tuple(g[m * lanes:(m + 1) * lanes, :] for g in go_parts), NN
        )
        gr = part if gr is None else gr + part
    for j in range(right_count):
        gr_ref[pl.ds(j, share, stride=right_count), :] = gr[:, j * width:(j + 1) * width]

    second.wait_recv()
    second.wait_send()
    total = gwf[...] + gwx[...]
    gwo[core] = total
    half = total.shape[0]
    third = remote(gwo.at[core], gwo.at[core], as_sem.at[2], ar_sem.at[2], row, mate)
    third.start()

    loads[3].wait()
    for k in range(1, n):
        at = rows_of(k)
        pltpu.make_async_copy(pairb.at[at], pairb.at[at], pr_sem.at[at]).wait()
    pair = pairs[:, own_rows, :] + bv[...]
    for k in range(1, n):
        pair += pairb[rows_of(k)]
    for j in range(right_count):
        pair_ref[pl.ds(j, left_count, stride=right_count), :] = pair[j]
    for k in range(1, n):
        at = cols_of(k)
        pltpu.make_async_copy(glb.at[at], glb.at[at], glr_sem.at[at]).wait()
    gl = gls[col]
    for k in range(1, n):
        gl += glb[cols_of(k)]
    for i in range(left_count):
        gl_ref[pl.ds(i, share, stride=left_count), :] = gl[:, i * width:(i + 1) * width]
    pltpu.make_async_copy(gwf, gwo.at[1 - core], ar_sem.at[2]).wait()
    gw_ref[...] = gwo[...].reshape(gw_ref.shape)

    for copy in sends:
        copy.wait_send()
    first.wait_send()
    third.wait_send()


def write_kernel(*refs):
    count = len(refs) // 2
    sems = refs[-1]
    copies = [
        pltpu.make_async_copy(refs[at], refs[count + at], sems.at[at]) for at in range(count)
    ]
    for copy in copies:
        copy.start()
    for copy in copies:
        copy.wait()


def fused(n, left_act, right_act, weight, bias, cotangent):
    share, right_count, width = right_act.shape
    left_count = cotangent.shape[0]
    pair_width = weight.shape[1]
    seqs = share * n
    f32, bf16 = jnp.float32, jnp.bfloat16
    block = width // n
    left_all = n * left_count
    left_lanes, right_lanes = left_count * width, right_count * width
    pairs = left_all * right_count
    half = block * width // 2
    dma = pltpu.SemaphoreType.DMA
    vmem = pl.BlockSpec(memory_space=pltpu.VMEM)
    hbm = pl.BlockSpec(memory_space=pltpu.HBM)
    kept = pltpu.VMEM
    shapes = (
        (left_count * right_count, pair_width),
        (share * left_count, width),
        (share * right_count, width),
        (block * width, pair_width),
    )
    results = pl.pallas_call(
        functools.partial(fused_kernel, n, seqs, left_count, right_count, width, pair_width),
        out_shape=tuple(kept(s, f32) for s in shapes),
        in_specs=[hbm] * 5,
        out_specs=(vmem,) * 4,
        scratch_shapes=[
            kept((share * left_count, width), f32),
            kept((share * right_count, width), f32),
            kept(weight.shape, f32),
            kept((1, pair_width), f32),
            kept((share, left_lanes), f32),
            kept((share, right_lanes), f32),
            kept((n, left_count * block * share // LANES, LANES), f32),
            kept((n, left_count * block * share // LANES, LANES), f32),
            kept((left_count * block, seqs), f32),
            kept((block, left_count, seqs), f32),
            kept((block, left_all, seqs), f32),
            kept((n, share, left_lanes), f32),
            kept((n, share, right_lanes), f32),
            kept((left_all, right_count, pair_width), f32),
            kept(weight.shape, bf16),
            kept(weight.shape, bf16),
            kept((pairs, block * width), f32),
            kept((right_count, left_all, pair_width), f32),
            kept((n, right_count, left_count, pair_width), f32),
            kept((right_lanes // LANES, left_all * width, LANES), f32),
            kept((n, share, left_lanes), f32),
            kept((n, share, left_lanes), f32),
            kept((2, half, pair_width), f32),
            kept((half, pair_width), f32),
            kept((half, pair_width), f32),
            kept((half, pair_width), f32),
            kept((2, half, pair_width), f32),
            dma((5,)),
            dma((n - 1,)), dma((n,)), dma((n - 1,)), dma((n,)),
            dma((n - 1,)), dma((n,)), dma((n - 1,)), dma((n,)),
            dma((n - 1,)), dma((n,)), dma((n - 1,)), dma((n,)),
            dma((n - 1,)), dma((n,)), dma((3,)), dma((3,)),
        ],
        compiler_params=pltpu.CompilerParams(
            collective_id=0, has_side_effects=True, vmem_limit_bytes=40 * 2**20
        ),
    )(*(
        pltpu.with_memory_space_constraint(value, pltpu.HBM) for value in (
            left_act.reshape(share * left_count, width),
            right_act.reshape(share * right_count, width),
            weight,
            bias.reshape(1, pair_width),
            cotangent,
        )
    ))
    pair, gl, gr, gw = pl.pallas_call(
        write_kernel,
        out_shape=tuple(jax.ShapeDtypeStruct(s, f32) for s in shapes),
        in_specs=[vmem] * 4,
        out_specs=(hbm,) * 4,
        scratch_shapes=[dma((4,))],
    )(*(pltpu.with_memory_space_constraint(value, pltpu.VMEM) for value in results))
    return (
        pair.reshape(cotangent.shape),
        gl.reshape(left_act.shape),
        gr.reshape(right_act.shape),
        gw,
    )


def block_terms(left_block, right_full, cot_block, weight_cube, bias):
    seqs = right_full.shape[0]
    highest = lax.Precision.HIGHEST
    products = jnp.einsum("sic,sjd->icjd", left_block, right_full, precision=highest) / seqs
    pair_block = jnp.einsum("icjd,cdz->ijz", products, weight_cube, precision=highest) + bias
    grad_outer = jnp.einsum("ijz,cdz->icjd", cot_block, weight_cube, precision=highest)
    weight_term = jnp.einsum("icjd,ijz->cdz", products, cot_block, precision=highest)
    left_term = jnp.einsum("icjd,sjd->sic", grad_outer, right_full, precision=highest) / seqs
    right_term = jnp.einsum("icjd,sic->sjd", grad_outer, left_block, precision=highest) / seqs
    return (pair_block, weight_term, left_term, right_term)


def general(left_act, right_act, weight, bias, cotangent):
    width = left_act.shape[2]
    pair_width = weight.shape[1]
    widened = lax.all_gather(left_act, "col", axis=1, tiled=True)
    left_full = lax.all_to_all(widened, "row", split_axis=1, concat_axis=0, tiled=True)
    right_full = lax.all_gather(right_act, "row", axis=0, tiled=True)
    weight_cube = weight.reshape(width, width, pair_width)
    pair, grad_cube, left_partial, right_partial = block_terms(
        left_full, right_full, cotangent, weight_cube, bias
    )
    returned = lax.all_to_all(left_partial, "row", split_axis=0, concat_axis=1, tiled=True)
    grad_left = lax.psum_scatter(returned, "col", scatter_dimension=1, tiled=True)
    grad_right = lax.psum_scatter(right_partial, "row", scatter_dimension=0, tiled=True)
    grad_flat = grad_cube.reshape(width * width, pair_width)
    weight_part = lax.psum_scatter(grad_flat, "row", scatter_dimension=0, tiled=True)
    grad_weight = lax.psum(weight_part, "col")
    return (pair, grad_left, grad_right, grad_weight)


def shards(rows, cols, left_act, right_act, weight, bias, cotangent):
    share, right_count, width = right_act.shape
    left_count = cotangent.shape[0]
    fits = (
        rows == cols == 4
        and left_count == right_count == SUBLANES
        and share == width
        and share * rows == LANES
        and 4 * width == LANES
        and 4 * SUBLANES == width
        and weight.shape[1] == LANES
    )
    if fits:
        return fused(rows, left_act, right_act, weight, bias, cotangent)
    return general(left_act, right_act, weight, bias, cotangent)


def solution(mesh):
    placed = (
        P(("groups", "row"), "col", None),
        P(("groups", "row"), "col", None),
        P(),
        P(),
        P(("groups", "row"), "col", None),
    )
    return jax.shard_map(
        functools.partial(shards, mesh.shape["row"], mesh.shape["col"]),
        mesh=mesh,
        in_specs=placed,
        out_specs=(
            P(("groups", "row"), "col", None),
            P(("groups", "row"), "col", None),
            P(("groups", "row"), "col", None),
            P(("groups", "row"), None),
        ),
        check_vma=False,
    )
```

```python
import functools

import jax
import jax.numpy as jnp
from jax import lax
from jax.experimental import pallas as pl
from jax.experimental.pallas import tpu as pltpu
from jax.sharding import PartitionSpec as P

LANES = 128
SUBLANES = 8
NN = (((1,), (0,)), ((), ()))
NT = (((1,), (1,)), ((), ()))


def split(value):
    high = value.astype(jnp.bfloat16)
    low = (value - high.astype(jnp.float32)).astype(jnp.bfloat16)
    return high, low


def product(a, b, dims):
    dot = functools.partial(lax.dot_general, dimension_numbers=dims, preferred_element_type=jnp.float32)
    return dot(a[0], b[1]) + dot(a[1], b[0]) + dot(a[0], b[0])


def swap_groups(tiles, width):
    lane = lax.broadcasted_iota(jnp.int32, tiles[0].shape, 1)
    low_half = lane < 2 * width
    even = lax.rem(lane // width, 2) == 0
    x = list(tiles)
    for p in (0, 1):
        a, b = x[p], x[p + 2]
        x[p] = jnp.where(low_half, a, pltpu.roll(b, 2 * width, 1))
        x[p + 2] = jnp.where(low_half, pltpu.roll(a, 2 * width, 1), b)
    for p in (0, 2):
        a, b = x[p], x[p + 1]
        x[p] = jnp.where(even, a, pltpu.roll(b, width, 1))
        x[p + 1] = jnp.where(even, pltpu.roll(a, LANES - width, 1), b)
    return x


def fused_kernel(
    n, seqs, left_count, right_count, width, pair_width,
    l_hbm, r_hbm, w_hbm, b_hbm, c_hbm,
    pair_ref, gl_ref, gr_ref, gw_ref,
    lv, rv, wv, bv, lpack, rpack, lsend, lrecv, lmt, lmid, ltbuf, lrow, rbuf, cotbuf,
    whi, wlo, outer2, pairs, pairb, gop, gls, glb, gws, gwa, gwe, gwx, gwf, gwo,
    in_sem, ls_sem, lr_sem, rs_sem, rr_sem, cs_sem, cr_sem, rows_sem, rowr_sem,
    ms_sem, mr_sem, ps_sem, pr_sem, gls_sem, glr_sem, as_sem, ar_sem,
):
    group, row, col = lax.axis_index("groups"), lax.axis_index("row"), lax.axis_index("col")
    share = seqs // n
    quads = LANES // width
    block = width // n
    left_all = n * left_count
    halves = right_count // quads
    lanes_r = right_count * width
    core = lax.rem(col, 2)
    mate = col + 1 - 2 * core
    across = lax.rem(col + 2, n)
    others = (2, 1, 3)

    def remote(src, dst, send, recv, to_row, to_col):
        return pltpu.make_async_remote_copy(
            src_ref=src, dst_ref=dst, send_sem=send, recv_sem=recv,
            device_id=(group, to_row, to_col), device_id_type=pl.DeviceIdType.MESH,
        )

    def arrived(block, sem):
        pltpu.make_async_copy(block, block, sem).wait()

    def rows_of(k):
        return lax.rem(row + k, n)

    def cols_of(k):
        return lax.rem(col + k, n)

    own_rows = pl.ds(pl.multiple_of(row * left_count, left_count), left_count)
    own_cols = pl.ds(pl.multiple_of(col * left_count, left_count), left_count)
    loads = [
        pltpu.make_async_copy(src, dst, in_sem.at[at])
        for at, (src, dst) in enumerate(
            ((l_hbm, lv), (r_hbm, rv), (w_hbm, wv), (b_hbm, bv), (c_hbm, cotbuf.at[own_rows]))
        )
    ]
    loads[0].start()
    loads[1].start()
    barrier = pltpu.get_barrier_semaphore()
    for k in others:
        for to in ((rows_of(k), col), (row, cols_of(k))):
            pl.semaphore_signal(
                barrier, inc=1, device_id=(group,) + to, device_id_type=pl.DeviceIdType.MESH,
            )

    loads[0].wait()
    for i in range(left_count):
        lpack[:, i * width:(i + 1) * width] = lv[pl.ds(i, share, stride=left_count), :]
    loads[1].wait()
    for load in loads[2:]:
        load.start()
    for j in range(right_count):
        rpack[:, j * width:(j + 1) * width] = rv[pl.ds(j, share, stride=right_count), :]
    left_t = lpack[...].T
    for q in range(n):
        for i in range(left_count):
            hi, lo = i // quads, i % quads
            lsend[q, hi * block:(hi + 1) * block, lo * share:(lo + 1) * share] = (
                left_t[i * width + q * block:i * width + (q + 1) * block, :]
            )
    pl.semaphore_wait(barrier, 2 * (n - 1))

    sends = []

    def send(*args):
        copy = remote(*args)
        copy.start()
        sends.append(copy)

    for k in others:
        to = rows_of(k)
        send(lsend.at[to], lrecv.at[row], ls_sem.at[k - 1], lr_sem.at[row], to, col)
    for k in others:
        send(rpack, rbuf.at[row], rs_sem.at[k - 1], rr_sem.at[row], rows_of(k), col)
    for k in (1, 2, 3):
        send(lpack, lrow.at[col], rows_sem.at[k - 1], rowr_sem.at[col], row, cols_of(k))
    for k in (1, 2, 3):
        send(c_hbm, cotbuf.at[own_rows], cs_sem.at[k - 1], cr_sem.at[row], rows_of(k), col)
    lrecv[row] = lsend[row]
    rbuf[row] = rpack[...]
    lrow[col] = lpack[...]

    loads[2].wait()
    high, low = split(wv[...])
    whi[...] = high
    wlo[...] = low

    for k in range(1, n):
        at = rows_of(k)
        arrived(lsend.at[0], lr_sem.at[at])
    for hi in range(left_count // quads):
        tiles = [lrecv[k, hi * block:(hi + 1) * block, :] for k in range(n)]
        for lo, tile in enumerate(swap_groups(tiles, width)):
            at = (hi * quads + lo) * block
            lmt[at:at + block, :] = tile
    for c in range(block):
        lmid[c] = lmt[pl.ds(c, left_count, stride=block), :]
    for k in (1, 2, 3):
        send(lmid, ltbuf.at[:, own_cols], ms_sem.at[k - 1], mr_sem.at[col], row, cols_of(k))
    ltbuf[:, own_cols, :] = lmid[...]

    for k in range(1, n):
        at = rows_of(k)
        arrived(rpack, rr_sem.at[at])
    right_parts = split(rbuf[...].reshape(seqs, lanes_r))
    for k in range(1, n):
        at = cols_of(k)
        arrived(lmid, mr_sem.at[at])
    left_parts = split(ltbuf[...].reshape(block * left_all, seqs))
    outer = product(left_parts, right_parts, NN) * (1.0 / seqs)
    for m in range(n):
        for h in range(halves):
            for q in range(block // quads):
                tiles = []
                for a in range(quads):
                    at = ((q * quads + a) * n + m) * left_count
                    tiles.append(outer[at:at + left_count, h * LANES:(h + 1) * LANES])
                for b, tile in enumerate(swap_groups(tiles, width)):
                    at = ((h * quads + b) * n + m) * left_count
                    outer2[at:at + left_count, q * LANES:(q + 1) * LANES] = tile
    w_rows = pl.ds(pl.multiple_of(row * block * width, block * width), block * width)
    outer_parts = split(outer2[...])
    pairs[...] = product(outer_parts, (whi[w_rows, :], wlo[w_rows, :]), NN).reshape(pairs.shape)
    for k in (1, 2, 3):
        to = rows_of(k)
        piece = pl.ds(pl.multiple_of(to * left_count, left_count), left_count)
        send(pairs.at[:, piece], pairb.at[row], ps_sem.at[k - 1], pr_sem.at[row], to, col)
    outer_t = split(outer2[...].T)

    loads[4].wait()
    for k in range(1, n):
        at = rows_of(k)
        arrived(c_hbm, cr_sem.at[at])
    cot = jnp.concatenate(
        [cotbuf[:, j, :] for j in range(right_count)], axis=0
    )
    cot_parts = split(cot)
    gws[...] = product(outer_t, cot_parts, NN).reshape(gws.shape)
    first = remote(gws.at[1 - core], gwa, as_sem.at[0], ar_sem.at[0], row, mate)
    first.start()
    ahead = gwa.shape[0] * 1 // 2
    early, late = pl.ds(0, ahead), pl.ds(ahead, gwa.shape[0] - ahead)
    diagonal = n - 1 - col
    straight = remote(
        gws.at[core, early], gwe.at[0, early], as_sem.at[3], ar_sem.at[3], row, across
    )
    skew = remote(
        gws.at[1 - core, early], gwe.at[1, early], as_sem.at[4], ar_sem.at[4], row, diagonal
    )
    straight.start()
    skew.start()

    go2 = product(cot_parts, (whi[...], wlo[...]), NT) * (1.0 / seqs)
    for m in range(n):
        for h in range(halves):
            for q in range(width // quads):
                tiles = []
                for b in range(quads):
                    at = ((h * quads + b) * n + m) * left_count
                    tiles.append(go2[at:at + left_count, q * LANES:(q + 1) * LANES])
                for a, tile in enumerate(swap_groups(tiles, width)):
                    at = (m * width + q * quads + a) * left_count
                    gop[h, at:at + left_count, :] = tile

    first.wait_recv()
    gwf[...] = gws[core] + gwa[...]
    second = remote(gwf.at[late], gwx.at[late], as_sem.at[1], ar_sem.at[1], row, across)
    second.start()

    grad_outer = jnp.concatenate(
        [
            jnp.concatenate(
                [
                    gop[h, pl.ds(m * width * left_count + i, width, stride=left_count), :]
                    for m in range(n) for i in range(left_count)
                ],
                axis=0,
            )
            for h in range(halves)
        ],
        axis=1,
    )
    go_parts = split(grad_outer)
    own_parts = split(rpack[...])
    gl_part = product(own_parts, go_parts, NT)
    for m in range(n):
        gls[m] = gl_part[:, m * left_count * width:(m + 1) * left_count * width]
    for k in (1, 2, 3):
        to = cols_of(k)
        send(gls.at[to], glb.at[col], gls_sem.at[k - 1], glr_sem.at[col], row, to)

    for k in range(1, n):
        at = cols_of(k)
        arrived(lpack, rowr_sem.at[at])
    gr = None
    for m in range(n):
        lanes = left_count * width
        part = product(
            split(lrow[m]), tuple(g[m * lanes:(m + 1) * lanes, :] for g in go_parts), NN
        )
        gr = part if gr is None else gr + part
    for j in range(right_count):
        gr_ref[pl.ds(j, share, stride=right_count), :] = gr[:, j * width:(j + 1) * width]

    straight.wait()
    skew.wait()
    gwo[core, early] = gwf[early] + (gwe[0, early] + gwe[1, early])
    second.wait()
    gwo[core, late] = gwf[late] + gwx[late]
    third = remote(gwo.at[core], gwo.at[core], as_sem.at[2], ar_sem.at[2], row, mate)
    third.start()

    loads[3].wait()
    for k in range(1, n):
        at = rows_of(k)
        arrived(pairb.at[at], pr_sem.at[at])
    pair = pairs[:, own_rows, :] + bv[...]
    for k in range(1, n):
        pair += pairb[rows_of(k)]
    for j in range(right_count):
        pair_ref[pl.ds(j, left_count, stride=right_count), :] = pair[j]
    for k in range(1, n):
        at = cols_of(k)
        arrived(glb.at[at], glr_sem.at[at])
    gl = gls[col]
    for k in range(1, n):
        gl += glb[cols_of(k)]
    for i in range(left_count):
        gl_ref[pl.ds(i, share, stride=left_count), :] = gl[:, i * width:(i + 1) * width]
    for copy in sends:
        copy.wait_send()
    arrived(gwf, ar_sem.at[2])
    gw_ref[...] = gwo[...].reshape(gw_ref.shape)

    first.wait_send()
    third.wait_send()


def write_kernel(*refs):
    count = len(refs) // 2
    sems = refs[-1]
    copies = [
        pltpu.make_async_copy(refs[at], refs[count + at], sems.at[at]) for at in range(count)
    ]
    for copy in copies:
        copy.start()
    for copy in copies:
        copy.wait()


def fused(n, left_act, right_act, weight, bias, cotangent):
    share, right_count, width = right_act.shape
    left_count = cotangent.shape[0]
    pair_width = weight.shape[1]
    seqs = share * n
    f32, bf16 = jnp.float32, jnp.bfloat16
    block = width // n
    left_all = n * left_count
    left_lanes, right_lanes = left_count * width, right_count * width
    pairs = left_all * right_count
    half = block * width // 2
    dma = pltpu.SemaphoreType.DMA
    vmem = pl.BlockSpec(memory_space=pltpu.VMEM)
    hbm = pl.BlockSpec(memory_space=pltpu.HBM)
    kept = pltpu.VMEM
    shapes = (
        (left_count * right_count, pair_width),
        (share * left_count, width),
        (share * right_count, width),
        (block * width, pair_width),
    )
    results = pl.pallas_call(
        functools.partial(fused_kernel, n, seqs, left_count, right_count, width, pair_width),
        out_shape=tuple(kept(s, f32) for s in shapes),
        in_specs=[hbm] * 5,
        out_specs=(vmem,) * 4,
        scratch_shapes=[
            kept((share * left_count, width), f32),
            kept((share * right_count, width), f32),
            kept(weight.shape, f32),
            kept((1, pair_width), f32),
            kept((share, left_lanes), f32),
            kept((share, right_lanes), f32),
            kept((n, left_count * block * share // LANES, LANES), f32),
            kept((n, left_count * block * share // LANES, LANES), f32),
            kept((left_count * block, seqs), f32),
            kept((block, left_count, seqs), f32),
            kept((block, left_all, seqs), f32),
            kept((n, share, left_lanes), f32),
            kept((n, share, right_lanes), f32),
            kept((left_all, right_count, pair_width), f32),
            kept(weight.shape, bf16),
            kept(weight.shape, bf16),
            kept((pairs, block * width), f32),
            kept((right_count, left_all, pair_width), f32),
            kept((n, right_count, left_count, pair_width), f32),
            kept((right_lanes // LANES, left_all * width, LANES), f32),
            kept((n, share, left_lanes), f32),
            kept((n, share, left_lanes), f32),
            kept((2, half, pair_width), f32),
            kept((half, pair_width), f32),
            kept((2, half, pair_width), f32),
            kept((half, pair_width), f32),
            kept((half, pair_width), f32),
            kept((2, half, pair_width), f32),
            dma((5,)),
            dma((n,)), dma((n,)), dma((n,)), dma((n,)),
            dma((n,)), dma((n,)), dma((n,)), dma((n,)),
            dma((n,)), dma((n,)), dma((n,)), dma((n,)),
            dma((n,)), dma((n,)), dma((5,)), dma((5,)),
        ],
        compiler_params=pltpu.CompilerParams(
            collective_id=0, has_side_effects=True, vmem_limit_bytes=40 * 2**20
        ),
    )(*(
        pltpu.with_memory_space_constraint(value, pltpu.HBM) for value in (
            left_act.reshape(share * left_count, width),
            right_act.reshape(share * right_count, width),
            weight,
            bias.reshape(1, pair_width),
            cotangent,
        )
    ))
    pair, gl, gr, gw = pl.pallas_call(
        write_kernel,
        out_shape=tuple(jax.ShapeDtypeStruct(s, f32) for s in shapes),
        in_specs=[vmem] * 4,
        out_specs=(hbm,) * 4,
        scratch_shapes=[dma((4,))],
    )(*(pltpu.with_memory_space_constraint(value, pltpu.VMEM) for value in results))
    return (
        pair.reshape(cotangent.shape),
        gl.reshape(left_act.shape),
        gr.reshape(right_act.shape),
        gw,
    )


def block_terms(left_block, right_full, cot_block, weight_cube, bias):
    seqs = right_full.shape[0]
    highest = lax.Precision.HIGHEST
    products = jnp.einsum("sic,sjd->icjd", left_block, right_full, precision=highest) / seqs
    pair_block = jnp.einsum("icjd,cdz->ijz", products, weight_cube, precision=highest) + bias
    grad_outer = jnp.einsum("ijz,cdz->icjd", cot_block, weight_cube, precision=highest)
    weight_term = jnp.einsum("icjd,ijz->cdz", products, cot_block, precision=highest)
    left_term = jnp.einsum("icjd,sjd->sic", grad_outer, right_full, precision=highest) / seqs
    right_term = jnp.einsum("icjd,sic->sjd", grad_outer, left_block, precision=highest) / seqs
    return (pair_block, weight_term, left_term, right_term)


def general(left_act, right_act, weight, bias, cotangent):
    width = left_act.shape[2]
    pair_width = weight.shape[1]
    widened = lax.all_gather(left_act, "col", axis=1, tiled=True)
    left_full = lax.all_to_all(widened, "row", split_axis=1, concat_axis=0, tiled=True)
    right_full = lax.all_gather(right_act, "row", axis=0, tiled=True)
    weight_cube = weight.reshape(width, width, pair_width)
    pair, grad_cube, left_partial, right_partial = block_terms(
        left_full, right_full, cotangent, weight_cube, bias
    )
    returned = lax.all_to_all(left_partial, "row", split_axis=0, concat_axis=1, tiled=True)
    grad_left = lax.psum_scatter(returned, "col", scatter_dimension=1, tiled=True)
    grad_right = lax.psum_scatter(right_partial, "row", scatter_dimension=0, tiled=True)
    grad_flat = grad_cube.reshape(width * width, pair_width)
    weight_part = lax.psum_scatter(grad_flat, "row", scatter_dimension=0, tiled=True)
    grad_weight = lax.psum(weight_part, "col")
    return (pair, grad_left, grad_right, grad_weight)


def shards(rows, cols, left_act, right_act, weight, bias, cotangent):
    share, right_count, width = right_act.shape
    left_count = cotangent.shape[0]
    fits = (
        rows == cols == 4
        and left_count == right_count == SUBLANES
        and share == width
        and share * rows == LANES
        and 4 * width == LANES
        and 4 * SUBLANES == width
        and weight.shape[1] == LANES
    )
    if fits:
        return fused(rows, left_act, right_act, weight, bias, cotangent)
    return general(left_act, right_act, weight, bias, cotangent)


def solution(mesh):
    placed = (
        P(("groups", "row"), "col", None),
        P(("groups", "row"), "col", None),
        P(),
        P(),
        P(("groups", "row"), "col", None),
    )
    return jax.shard_map(
        functools.partial(shards, mesh.shape["row"], mesh.shape["col"]),
        mesh=mesh,
        in_specs=placed,
        out_specs=(
            P(("groups", "row"), "col", None),
            P(("groups", "row"), "col", None),
            P(("groups", "row"), "col", None),
            P(("groups", "row"), None),
        ),
        check_vma=False,
    )
```

```python
import functools

import jax
import jax.numpy as jnp
from jax import lax
from jax.experimental import pallas as pl
from jax.experimental.pallas import tpu as pltpu
from jax.sharding import PartitionSpec as P

LANES = 128
SUBLANES = 8
NN = (((1,), (0,)), ((), ()))
NT = (((1,), (1,)), ((), ()))


def split(value):
    high = value.astype(jnp.bfloat16)
    low = (value - high.astype(jnp.float32)).astype(jnp.bfloat16)
    return high, low


def product(a, b, dims):
    dot = functools.partial(lax.dot_general, dimension_numbers=dims, preferred_element_type=jnp.float32)
    return dot(a[0], b[1]) + dot(a[1], b[0]) + dot(a[0], b[0])


def swap_groups(tiles, width):
    lane = lax.broadcasted_iota(jnp.int32, tiles[0].shape, 1)
    low_half = lane < 2 * width
    even = lax.rem(lane // width, 2) == 0
    x = list(tiles)
    for p in (0, 1):
        a, b = x[p], x[p + 2]
        x[p] = jnp.where(low_half, a, pltpu.roll(b, 2 * width, 1))
        x[p + 2] = jnp.where(low_half, pltpu.roll(a, 2 * width, 1), b)
    for p in (0, 2):
        a, b = x[p], x[p + 1]
        x[p] = jnp.where(even, a, pltpu.roll(b, width, 1))
        x[p + 1] = jnp.where(even, pltpu.roll(a, LANES - width, 1), b)
    return x


def fused_kernel(
    n, seqs, left_count, right_count, width, pair_width,
    l_hbm, r_hbm, w_hbm, b_hbm, c_hbm,
    pair_ref, gl_ref, gr_ref, gw_ref,
    lv, rv, wv, bv, lpack, rpack, lsend, lrecv, lmt, lmid, ltbuf, lrow, rbuf, cotbuf,
    whi, wlo, outer2, pairs, pairb, gop, gls, glb, gws, gwa, gwe, gwx, gwf, gwo,
    in_sem, ls_sem, lr_sem, rs_sem, rr_sem, cs_sem, cr_sem, rows_sem, rowr_sem,
    ms_sem, mr_sem, ps_sem, pr_sem, gls_sem, glr_sem, as_sem, ar_sem,
):
    group, row, col = lax.axis_index("groups"), lax.axis_index("row"), lax.axis_index("col")
    share = seqs // n
    quads = LANES // width
    block = width // n
    left_all = n * left_count
    halves = right_count // quads
    lanes_r = right_count * width
    core = lax.rem(col, 2)
    mate = col + 1 - 2 * core
    across = lax.rem(col + 2, n)
    others = (2, 1, 3)

    def remote(src, dst, send, recv, to_row, to_col):
        return pltpu.make_async_remote_copy(
            src_ref=src, dst_ref=dst, send_sem=send, recv_sem=recv,
            device_id=(group, to_row, to_col), device_id_type=pl.DeviceIdType.MESH,
        )

    def arrived(block, sem):
        pltpu.make_async_copy(block, block, sem).wait()

    def rows_of(k):
        return lax.rem(row + k, n)

    def cols_of(k):
        return lax.rem(col + k, n)

    own_rows = pl.ds(pl.multiple_of(row * left_count, left_count), left_count)
    own_cols = pl.ds(pl.multiple_of(col * left_count, left_count), left_count)
    loads = [
        pltpu.make_async_copy(src, dst, in_sem.at[at])
        for at, (src, dst) in enumerate(
            ((l_hbm, lv), (r_hbm, rv), (w_hbm, wv), (b_hbm, bv), (c_hbm, cotbuf.at[own_rows]))
        )
    ]
    loads[0].start()
    loads[1].start()
    barrier = pltpu.get_barrier_semaphore()
    for k in others:
        for to in ((rows_of(k), col), (row, cols_of(k))):
            pl.semaphore_signal(
                barrier, inc=1, device_id=(group,) + to, device_id_type=pl.DeviceIdType.MESH,
            )

    loads[0].wait()
    for i in range(left_count):
        lpack[:, i * width:(i + 1) * width] = lv[pl.ds(i, share, stride=left_count), :]
    loads[1].wait()
    for load in loads[2:]:
        load.start()
    for j in range(right_count):
        rpack[:, j * width:(j + 1) * width] = rv[pl.ds(j, share, stride=right_count), :]
    left_t = lpack[...].T
    for q in range(n):
        for i in range(left_count):
            hi, lo = i // quads, i % quads
            lsend[q, hi * block:(hi + 1) * block, lo * share:(lo + 1) * share] = (
                left_t[i * width + q * block:i * width + (q + 1) * block, :]
            )
    pl.semaphore_wait(barrier, 2 * (n - 1))

    sends = []

    def send(*args):
        copy = remote(*args)
        copy.start()
        sends.append(copy)

    for k in others:
        to = rows_of(k)
        send(lsend.at[to], lrecv.at[row], ls_sem.at[k - 1], lr_sem.at[row], to, col)
    for k in others:
        send(rpack, rbuf.at[row], rs_sem.at[k - 1], rr_sem.at[row], rows_of(k), col)
    for k in (1, 2, 3):
        send(lpack, lrow.at[col], rows_sem.at[k - 1], rowr_sem.at[col], row, cols_of(k))
    for k in (1, 2, 3):
        send(c_hbm, cotbuf.at[own_rows], cs_sem.at[k - 1], cr_sem.at[row], rows_of(k), col)
    lrecv[row] = lsend[row]
    rbuf[row] = rpack[...]
    lrow[col] = lpack[...]

    loads[2].wait()
    high, low = split(wv[...])
    whi[...] = high
    wlo[...] = low

    for k in range(1, n):
        at = rows_of(k)
        arrived(lsend.at[0], lr_sem.at[at])
    for hi in range(left_count // quads):
        tiles = [lrecv[k, hi * block:(hi + 1) * block, :] for k in range(n)]
        for lo, tile in enumerate(swap_groups(tiles, width)):
            at = (hi * quads + lo) * block
            lmt[at:at + block, :] = tile
    for c in range(block):
        lmid[c] = lmt[pl.ds(c, left_count, stride=block), :]
    for k in (1, 2, 3):
        send(lmid, ltbuf.at[:, own_cols], ms_sem.at[k - 1], mr_sem.at[col], row, cols_of(k))
    ltbuf[:, own_cols, :] = lmid[...]

    for k in range(1, n):
        at = rows_of(k)
        arrived(rpack, rr_sem.at[at])
    right_parts = split(rbuf[...].reshape(seqs, lanes_r))
    for k in range(1, n):
        at = cols_of(k)
        arrived(lmid, mr_sem.at[at])
    left_parts = split(ltbuf[...].reshape(block * left_all, seqs))
    outer = product(left_parts, right_parts, NN) * (1.0 / seqs)
    for m in range(n):
        for h in range(halves):
            for q in range(block // quads):
                tiles = []
                for a in range(quads):
                    at = ((q * quads + a) * n + m) * left_count
                    tiles.append(outer[at:at + left_count, h * LANES:(h + 1) * LANES])
                for b, tile in enumerate(swap_groups(tiles, width)):
                    at = ((h * quads + b) * n + m) * left_count
                    outer2[at:at + left_count, q * LANES:(q + 1) * LANES] = tile
    w_rows = pl.ds(pl.multiple_of(row * block * width, block * width), block * width)
    outer_parts = split(outer2[...])
    pairs[...] = product(outer_parts, (whi[w_rows, :], wlo[w_rows, :]), NN).reshape(pairs.shape)
    for k in (1, 2, 3):
        to = rows_of(k)
        piece = pl.ds(pl.multiple_of(to * left_count, left_count), left_count)
        send(pairs.at[:, piece], pairb.at[row], ps_sem.at[k - 1], pr_sem.at[row], to, col)
    outer_t = split(outer2[...].T)

    loads[4].wait()
    for k in range(1, n):
        at = rows_of(k)
        arrived(c_hbm, cr_sem.at[at])
    cot = jnp.concatenate(
        [cotbuf[:, j, :] for j in range(right_count)], axis=0
    )
    cot_parts = split(cot)
    gws[...] = product(outer_t, cot_parts, NN).reshape(gws.shape)
    first = remote(gws.at[1 - core], gwa, as_sem.at[0], ar_sem.at[0], row, mate)
    first.start()
    ahead = gwa.shape[0] * 1 // 2
    early, late = pl.ds(0, ahead), pl.ds(ahead, gwa.shape[0] - ahead)
    diagonal = n - 1 - col
    straight = remote(
        gws.at[core, early], gwe.at[0, early], as_sem.at[3], ar_sem.at[3], row, across
    )
    skew = remote(
        gws.at[1 - core, early], gwe.at[1, early], as_sem.at[4], ar_sem.at[4], row, diagonal
    )
    straight.start()
    skew.start()

    go2 = product(cot_parts, (whi[...], wlo[...]), NT) * (1.0 / seqs)
    for m in range(n):
        for h in range(halves):
            for q in range(width // quads):
                tiles = []
                for b in range(quads):
                    at = ((h * quads + b) * n + m) * left_count
                    tiles.append(go2[at:at + left_count, q * LANES:(q + 1) * LANES])
                for a, tile in enumerate(swap_groups(tiles, width)):
                    at = (m * width + q * quads + a) * left_count
                    gop[h, at:at + left_count, :] = tile

    first.wait_recv()
    gwf[...] = gws[core] + gwa[...]
    second = remote(gwf.at[late], gwx.at[late], as_sem.at[1], ar_sem.at[1], row, across)
    second.start()

    own_parts = split(rpack[...])
    go_parts, gl_out = [], []
    for m in range(n):
        grad_outer = jnp.concatenate(
            [
                jnp.concatenate(
                    [
                        gop[h, pl.ds(m * width * left_count + i, width, stride=left_count), :]
                        for i in range(left_count)
                    ],
                    axis=0,
                )
                for h in range(halves)
            ],
            axis=1,
        )
        go_parts.append(split(grad_outer))
        gls[m] = product(own_parts, go_parts[m], NT)
        gl_out.append(remote(gls.at[m], glb.at[col], gls_sem.at[m], glr_sem.at[col], row, m))

        @pl.when(col != m)
        def _():
            gl_out[m].start()

    for k in range(1, n):
        at = cols_of(k)
        arrived(lpack, rowr_sem.at[at])
    gr = None
    for m in range(n):
        part = product(split(lrow[m]), go_parts[m], NN)
        gr = part if gr is None else gr + part
    for j in range(right_count):
        gr_ref[pl.ds(j, share, stride=right_count), :] = gr[:, j * width:(j + 1) * width]

    straight.wait()
    skew.wait()
    gwo[core, early] = gwf[early] + (gwe[0, early] + gwe[1, early])
    second.wait()
    gwo[core, late] = gwf[late] + gwx[late]
    third = remote(gwo.at[core], gwo.at[core], as_sem.at[2], ar_sem.at[2], row, mate)
    third.start()

    loads[3].wait()
    for k in range(1, n):
        at = rows_of(k)
        arrived(pairb.at[at], pr_sem.at[at])
    pair = pairs[:, own_rows, :] + bv[...]
    for k in range(1, n):
        pair += pairb[rows_of(k)]
    for j in range(right_count):
        pair_ref[pl.ds(j, left_count, stride=right_count), :] = pair[j]
    for k in range(1, n):
        at = cols_of(k)
        arrived(glb.at[at], glr_sem.at[at])
    gl = gls[col]
    for k in range(1, n):
        gl += glb[cols_of(k)]
    for i in range(left_count):
        gl_ref[pl.ds(i, share, stride=left_count), :] = gl[:, i * width:(i + 1) * width]
    for copy in sends:
        copy.wait_send()
    for m in range(n):
        @pl.when(col != m)
        def _():
            gl_out[m].wait_send()

    arrived(gwf, ar_sem.at[2])
    gw_ref[...] = gwo[...].reshape(gw_ref.shape)

    first.wait_send()
    third.wait_send()


def write_kernel(*refs):
    count = len(refs) // 2
    sems = refs[-1]
    copies = [
        pltpu.make_async_copy(refs[at], refs[count + at], sems.at[at]) for at in range(count)
    ]
    for copy in copies:
        copy.start()
    for copy in copies:
        copy.wait()


def fused(n, left_act, right_act, weight, bias, cotangent):
    share, right_count, width = right_act.shape
    left_count = cotangent.shape[0]
    pair_width = weight.shape[1]
    seqs = share * n
    f32, bf16 = jnp.float32, jnp.bfloat16
    block = width // n
    left_all = n * left_count
    left_lanes, right_lanes = left_count * width, right_count * width
    pairs = left_all * right_count
    half = block * width // 2
    dma = pltpu.SemaphoreType.DMA
    vmem = pl.BlockSpec(memory_space=pltpu.VMEM)
    hbm = pl.BlockSpec(memory_space=pltpu.HBM)
    kept = pltpu.VMEM
    shapes = (
        (left_count * right_count, pair_width),
        (share * left_count, width),
        (share * right_count, width),
        (block * width, pair_width),
    )
    results = pl.pallas_call(
        functools.partial(fused_kernel, n, seqs, left_count, right_count, width, pair_width),
        out_shape=tuple(kept(s, f32) for s in shapes),
        in_specs=[hbm] * 5,
        out_specs=(vmem,) * 4,
        scratch_shapes=[
            kept((share * left_count, width), f32),
            kept((share * right_count, width), f32),
            kept(weight.shape, f32),
            kept((1, pair_width), f32),
            kept((share, left_lanes), f32),
            kept((share, right_lanes), f32),
            kept((n, left_count * block * share // LANES, LANES), f32),
            kept((n, left_count * block * share // LANES, LANES), f32),
            kept((left_count * block, seqs), f32),
            kept((block, left_count, seqs), f32),
            kept((block, left_all, seqs), f32),
            kept((n, share, left_lanes), f32),
            kept((n, share, right_lanes), f32),
            kept((left_all, right_count, pair_width), f32),
            kept(weight.shape, bf16),
            kept(weight.shape, bf16),
            kept((pairs, block * width), f32),
            kept((right_count, left_all, pair_width), f32),
            kept((n, right_count, left_count, pair_width), f32),
            kept((right_lanes // LANES, left_all * width, LANES), f32),
            kept((n, share, left_lanes), f32),
            kept((n, share, left_lanes), f32),
            kept((2, half, pair_width), f32),
            kept((half, pair_width), f32),
            kept((2, half, pair_width), f32),
            kept((half, pair_width), f32),
            kept((half, pair_width), f32),
            kept((2, half, pair_width), f32),
            dma((5,)),
            dma((n,)), dma((n,)), dma((n,)), dma((n,)),
            dma((n,)), dma((n,)), dma((n,)), dma((n,)),
            dma((n,)), dma((n,)), dma((n,)), dma((n,)),
            dma((n,)), dma((n,)), dma((5,)), dma((5,)),
        ],
        compiler_params=pltpu.CompilerParams(
            collective_id=0, has_side_effects=True, vmem_limit_bytes=40 * 2**20
        ),
    )(*(
        pltpu.with_memory_space_constraint(value, pltpu.HBM) for value in (
            left_act.reshape(share * left_count, width),
            right_act.reshape(share * right_count, width),
            weight,
            bias.reshape(1, pair_width),
            cotangent,
        )
    ))
    pair, gl, gr, gw = pl.pallas_call(
        write_kernel,
        out_shape=tuple(jax.ShapeDtypeStruct(s, f32) for s in shapes),
        in_specs=[vmem] * 4,
        out_specs=(hbm,) * 4,
        scratch_shapes=[dma((4,))],
    )(*(pltpu.with_memory_space_constraint(value, pltpu.VMEM) for value in results))
    return (
        pair.reshape(cotangent.shape),
        gl.reshape(left_act.shape),
        gr.reshape(right_act.shape),
        gw,
    )


def block_terms(left_block, right_full, cot_block, weight_cube, bias):
    seqs = right_full.shape[0]
    highest = lax.Precision.HIGHEST
    products = jnp.einsum("sic,sjd->icjd", left_block, right_full, precision=highest) / seqs
    pair_block = jnp.einsum("icjd,cdz->ijz", products, weight_cube, precision=highest) + bias
    grad_outer = jnp.einsum("ijz,cdz->icjd", cot_block, weight_cube, precision=highest)
    weight_term = jnp.einsum("icjd,ijz->cdz", products, cot_block, precision=highest)
    left_term = jnp.einsum("icjd,sjd->sic", grad_outer, right_full, precision=highest) / seqs
    right_term = jnp.einsum("icjd,sic->sjd", grad_outer, left_block, precision=highest) / seqs
    return (pair_block, weight_term, left_term, right_term)


def general(left_act, right_act, weight, bias, cotangent):
    width = left_act.shape[2]
    pair_width = weight.shape[1]
    widened = lax.all_gather(left_act, "col", axis=1, tiled=True)
    left_full = lax.all_to_all(widened, "row", split_axis=1, concat_axis=0, tiled=True)
    right_full = lax.all_gather(right_act, "row", axis=0, tiled=True)
    weight_cube = weight.reshape(width, width, pair_width)
    pair, grad_cube, left_partial, right_partial = block_terms(
        left_full, right_full, cotangent, weight_cube, bias
    )
    returned = lax.all_to_all(left_partial, "row", split_axis=0, concat_axis=1, tiled=True)
    grad_left = lax.psum_scatter(returned, "col", scatter_dimension=1, tiled=True)
    grad_right = lax.psum_scatter(right_partial, "row", scatter_dimension=0, tiled=True)
    grad_flat = grad_cube.reshape(width * width, pair_width)
    weight_part = lax.psum_scatter(grad_flat, "row", scatter_dimension=0, tiled=True)
    grad_weight = lax.psum(weight_part, "col")
    return (pair, grad_left, grad_right, grad_weight)


def shards(rows, cols, left_act, right_act, weight, bias, cotangent):
    share, right_count, width = right_act.shape
    left_count = cotangent.shape[0]
    fits = (
        rows == cols == 4
        and left_count == right_count == SUBLANES
        and share == width
        and share * rows == LANES
        and 4 * width == LANES
        and 4 * SUBLANES == width
        and weight.shape[1] == LANES
    )
    if fits:
        return fused(rows, left_act, right_act, weight, bias, cotangent)
    return general(left_act, right_act, weight, bias, cotangent)


def solution(mesh):
    placed = (
        P(("groups", "row"), "col", None),
        P(("groups", "row"), "col", None),
        P(),
        P(),
        P(("groups", "row"), "col", None),
    )
    return jax.shard_map(
        functools.partial(shards, mesh.shape["row"], mesh.shape["col"]),
        mesh=mesh,
        in_specs=placed,
        out_specs=(
            P(("groups", "row"), "col", None),
            P(("groups", "row"), "col", None),
            P(("groups", "row"), "col", None),
            P(("groups", "row"), None),
        ),
        check_vma=False,
    )
```

```python
import functools

import jax
import jax.numpy as jnp
from jax import lax
from jax.experimental import pallas as pl
from jax.experimental.pallas import tpu as pltpu
from jax.sharding import PartitionSpec as P

LANES = 128
SUBLANES = 8
NN = (((1,), (0,)), ((), ()))
NT = (((1,), (1,)), ((), ()))


def split(value):
    high = value.astype(jnp.bfloat16)
    low = (value - high.astype(jnp.float32)).astype(jnp.bfloat16)
    return high, low


def product(a, b, dims):
    dot = functools.partial(lax.dot_general, dimension_numbers=dims, preferred_element_type=jnp.float32)
    return dot(a[0], b[1]) + dot(a[1], b[0]) + dot(a[0], b[0])


def swap_groups(tiles, width):
    lane = lax.broadcasted_iota(jnp.int32, tiles[0].shape, 1)
    low_half = lane < 2 * width
    even = lax.rem(lane // width, 2) == 0
    x = list(tiles)
    for p in (0, 1):
        a, b = x[p], x[p + 2]
        x[p] = jnp.where(low_half, a, pltpu.roll(b, 2 * width, 1))
        x[p + 2] = jnp.where(low_half, pltpu.roll(a, 2 * width, 1), b)
    for p in (0, 2):
        a, b = x[p], x[p + 1]
        x[p] = jnp.where(even, a, pltpu.roll(b, width, 1))
        x[p + 1] = jnp.where(even, pltpu.roll(a, LANES - width, 1), b)
    return x


def fused_kernel(
    n, seqs, left_count, right_count, width, pair_width,
    l_hbm, r_hbm, w_hbm, b_hbm, c_hbm,
    pair_ref, gl_ref, gr_ref, gw_ref,
    lv, rv, wv, bv, lpack, rpack, lsend, lrecv, lmt, lmid, ltbuf, lrow, rbuf, cotbuf,
    whi, wlo, outer2, pairs, pairb, gop, gls, glb, gws, gwa, gwe, gwx, gwf, gwo,
    in_sem, ls_sem, lr_sem, rs_sem, rr_sem, cs_sem, cr_sem, rows_sem, rowr_sem,
    ms_sem, mr_sem, ps_sem, pr_sem, gls_sem, glr_sem, as_sem, ar_sem,
):
    group, row, col = lax.axis_index("groups"), lax.axis_index("row"), lax.axis_index("col")
    share = seqs // n
    quads = LANES // width
    block = width // n
    left_all = n * left_count
    halves = right_count // quads
    lanes_r = right_count * width
    core = lax.rem(col, 2)
    mate = col + 1 - 2 * core
    across = lax.rem(col + 2, n)
    others = (2, 1, 3)

    def remote(src, dst, send, recv, to_row, to_col):
        return pltpu.make_async_remote_copy(
            src_ref=src, dst_ref=dst, send_sem=send, recv_sem=recv,
            device_id=(group, to_row, to_col), device_id_type=pl.DeviceIdType.MESH,
        )

    def arrived(block, sem):
        pltpu.make_async_copy(block, block, sem).wait()

    def rows_of(k):
        return lax.rem(row + k, n)

    def cols_of(k):
        return lax.rem(col + k, n)

    own_rows = pl.ds(pl.multiple_of(row * left_count, left_count), left_count)
    own_cols = pl.ds(pl.multiple_of(col * left_count, left_count), left_count)
    loads = [
        pltpu.make_async_copy(src, dst, in_sem.at[at])
        for at, (src, dst) in enumerate(
            ((l_hbm, lv), (r_hbm, rv), (w_hbm, wv), (b_hbm, bv), (c_hbm, cotbuf.at[own_rows]))
        )
    ]
    loads[0].start()
    loads[1].start()
    barrier = pltpu.get_barrier_semaphore()
    for k in others:
        for to in ((rows_of(k), col), (row, cols_of(k))):
            pl.semaphore_signal(
                barrier, inc=1, device_id=(group,) + to, device_id_type=pl.DeviceIdType.MESH,
            )

    loads[0].wait()
    for i in range(left_count):
        lpack[:, i * width:(i + 1) * width] = lv[pl.ds(i, share, stride=left_count), :]
    loads[1].wait()
    for load in loads[2:]:
        load.start()
    for j in range(right_count):
        rpack[:, j * width:(j + 1) * width] = rv[pl.ds(j, share, stride=right_count), :]
    left_t = lpack[...].T
    for q in range(n):
        for i in range(left_count):
            hi, lo = i // quads, i % quads
            lsend[q, hi * block:(hi + 1) * block, lo * share:(lo + 1) * share] = (
                left_t[i * width + q * block:i * width + (q + 1) * block, :]
            )
    pl.semaphore_wait(barrier, 2 * (n - 1))

    sends = []

    def send(*args):
        copy = remote(*args)
        copy.start()
        sends.append(copy)

    for k in others:
        to = rows_of(k)
        send(lsend.at[to], lrecv.at[row], ls_sem.at[k - 1], lr_sem.at[row], to, col)
    for k in others:
        send(rpack, rbuf.at[row], rs_sem.at[k - 1], rr_sem.at[row], rows_of(k), col)
    for k in (1, 2, 3):
        send(lpack, lrow.at[col], rows_sem.at[k - 1], rowr_sem.at[col], row, cols_of(k))
    for k in (1, 2, 3):
        send(c_hbm, cotbuf.at[own_rows], cs_sem.at[k - 1], cr_sem.at[row], rows_of(k), col)
    lrecv[row] = lsend[row]
    rbuf[row] = rpack[...]
    lrow[col] = lpack[...]

    loads[2].wait()
    high, low = split(wv[...])
    whi[...] = high
    wlo[...] = low

    for k in range(1, n):
        at = rows_of(k)
        arrived(lsend.at[0], lr_sem.at[at])
    for hi in range(left_count // quads):
        tiles = [lrecv[k, hi * block:(hi + 1) * block, :] for k in range(n)]
        for lo, tile in enumerate(swap_groups(tiles, width)):
            at = (hi * quads + lo) * block
            lmt[at:at + block, :] = tile
    for c in range(block):
        lmid[c] = lmt[pl.ds(c, left_count, stride=block), :]
    for k in (1, 2, 3):
        send(lmid, ltbuf.at[:, own_cols], ms_sem.at[k - 1], mr_sem.at[col], row, cols_of(k))
    ltbuf[:, own_cols, :] = lmid[...]

    for k in range(1, n):
        at = rows_of(k)
        arrived(rpack, rr_sem.at[at])
    right_parts = split(rbuf[...].reshape(seqs, lanes_r))
    for k in range(1, n):
        at = cols_of(k)
        arrived(lmid, mr_sem.at[at])
    left_parts = split(ltbuf[...].reshape(block * left_all, seqs))
    outer = product(left_parts, right_parts, NN) * (1.0 / seqs)
    for m in range(n):
        for h in range(halves):
            for q in range(block // quads):
                tiles = []
                for a in range(quads):
                    at = ((q * quads + a) * n + m) * left_count
                    tiles.append(outer[at:at + left_count, h * LANES:(h + 1) * LANES])
                for b, tile in enumerate(swap_groups(tiles, width)):
                    at = ((h * quads + b) * n + m) * left_count
                    outer2[at:at + left_count, q * LANES:(q + 1) * LANES] = tile
    w_rows = pl.ds(pl.multiple_of(row * block * width, block * width), block * width)
    outer_parts = split(outer2[...])
    pairs[...] = product(outer_parts, (whi[w_rows, :], wlo[w_rows, :]), NN).reshape(pairs.shape)
    for k in (1, 3, 2):
        to = rows_of(k)
        piece = pl.ds(pl.multiple_of(to * left_count, left_count), left_count)
        send(pairs.at[:, piece], pairb.at[row], ps_sem.at[k - 1], pr_sem.at[row], to, col)
    outer_t = split(outer2[...].T)

    loads[4].wait()
    for k in range(1, n):
        at = rows_of(k)
        arrived(c_hbm, cr_sem.at[at])
    cot = jnp.concatenate(
        [cotbuf[:, j, :] for j in range(right_count)], axis=0
    )
    cot_parts = split(cot)
    gws[...] = product(outer_t, cot_parts, NN).reshape(gws.shape)
    first = remote(gws.at[1 - core], gwa, as_sem.at[0], ar_sem.at[0], row, mate)
    ahead = gwa.shape[0] * 1 // 2
    early, late = pl.ds(0, ahead), pl.ds(ahead, gwa.shape[0] - ahead)
    diagonal = n - 1 - col
    straight = remote(
        gws.at[core, early], gwe.at[0, early], as_sem.at[3], ar_sem.at[3], row, across
    )
    skew = remote(
        gws.at[1 - core, early], gwe.at[1, early], as_sem.at[4], ar_sem.at[4], row, diagonal
    )
    straight.start()
    skew.start()
    first.start()

    go2 = product(cot_parts, (whi[...], wlo[...]), NT) * (1.0 / seqs)
    for m in range(n):
        for h in range(halves):
            for q in range(width // quads):
                tiles = []
                for b in range(quads):
                    at = ((h * quads + b) * n + m) * left_count
                    tiles.append(go2[at:at + left_count, q * LANES:(q + 1) * LANES])
                for a, tile in enumerate(swap_groups(tiles, width)):
                    at = (m * width + q * quads + a) * left_count
                    gop[h, at:at + left_count, :] = tile

    first.wait_recv()
    gwf[...] = gws[core] + gwa[...]
    second = remote(gwf.at[late], gwx.at[late], as_sem.at[1], ar_sem.at[1], row, across)
    second.start()

    grad_outer = jnp.concatenate(
        [
            jnp.concatenate(
                [
                    gop[h, pl.ds(m * width * left_count + i, width, stride=left_count), :]
                    for m in range(n) for i in range(left_count)
                ],
                axis=0,
            )
            for h in range(halves)
        ],
        axis=1,
    )
    go_parts = split(grad_outer)
    own_parts = split(rpack[...])
    gl_part = product(own_parts, go_parts, NT)
    for m in range(n):
        gls[m] = gl_part[:, m * left_count * width:(m + 1) * left_count * width]
    for k in (1, 2, 3):
        to = cols_of(k)
        send(gls.at[to], glb.at[col], gls_sem.at[k - 1], glr_sem.at[col], row, to)

    for k in range(1, n):
        at = cols_of(k)
        arrived(lpack, rowr_sem.at[at])
    gr = None
    for m in range(n):
        lanes = left_count * width
        part = product(
            split(lrow[m]), tuple(g[m * lanes:(m + 1) * lanes, :] for g in go_parts), NN
        )
        gr = part if gr is None else gr + part
    for j in range(right_count):
        gr_ref[pl.ds(j, share, stride=right_count), :] = gr[:, j * width:(j + 1) * width]

    straight.wait()
    skew.wait()
    gwo[core, early] = gwf[early] + (gwe[0, early] + gwe[1, early])
    second.wait()
    gwo[core, late] = gwf[late] + gwx[late]
    third = remote(gwo.at[core], gwo.at[core], as_sem.at[2], ar_sem.at[2], row, mate)
    third.start()

    for k in range(1, n):
        at = cols_of(k)
        arrived(glb.at[at], glr_sem.at[at])
    gl = gls[col]
    for k in range(1, n):
        gl += glb[cols_of(k)]
    for i in range(left_count):
        gl_ref[pl.ds(i, share, stride=left_count), :] = gl[:, i * width:(i + 1) * width]
    loads[3].wait()
    for k in range(1, n):
        at = rows_of(k)
        arrived(pairb.at[at], pr_sem.at[at])
    pair = pairs[:, own_rows, :] + bv[...]
    for k in range(1, n):
        pair += pairb[rows_of(k)]
    for j in range(right_count):
        pair_ref[pl.ds(j, left_count, stride=right_count), :] = pair[j]
    for copy in sends:
        copy.wait_send()
    arrived(gwf, ar_sem.at[2])
    gw_ref[...] = gwo[...].reshape(gw_ref.shape)

    first.wait_send()
    third.wait_send()


def write_kernel(*refs):
    count = len(refs) // 2
    sems = refs[-1]
    copies = [
        pltpu.make_async_copy(refs[at], refs[count + at], sems.at[at]) for at in range(count)
    ]
    for copy in copies:
        copy.start()
    for copy in copies:
        copy.wait()


def fused(n, left_act, right_act, weight, bias, cotangent):
    share, right_count, width = right_act.shape
    left_count = cotangent.shape[0]
    pair_width = weight.shape[1]
    seqs = share * n
    f32, bf16 = jnp.float32, jnp.bfloat16
    block = width // n
    left_all = n * left_count
    left_lanes, right_lanes = left_count * width, right_count * width
    pairs = left_all * right_count
    half = block * width // 2
    dma = pltpu.SemaphoreType.DMA
    vmem = pl.BlockSpec(memory_space=pltpu.VMEM)
    hbm = pl.BlockSpec(memory_space=pltpu.HBM)
    kept = pltpu.VMEM
    shapes = (
        (left_count * right_count, pair_width),
        (share * left_count, width),
        (share * right_count, width),
        (block * width, pair_width),
    )
    results = pl.pallas_call(
        functools.partial(fused_kernel, n, seqs, left_count, right_count, width, pair_width),
        out_shape=tuple(kept(s, f32) for s in shapes),
        in_specs=[hbm] * 5,
        out_specs=(vmem,) * 4,
        scratch_shapes=[
            kept((share * left_count, width), f32),
            kept((share * right_count, width), f32),
            kept(weight.shape, f32),
            kept((1, pair_width), f32),
            kept((share, left_lanes), f32),
            kept((share, right_lanes), f32),
            kept((n, left_count * block * share // LANES, LANES), f32),
            kept((n, left_count * block * share // LANES, LANES), f32),
            kept((left_count * block, seqs), f32),
            kept((block, left_count, seqs), f32),
            kept((block, left_all, seqs), f32),
            kept((n, share, left_lanes), f32),
            kept((n, share, right_lanes), f32),
            kept((left_all, right_count, pair_width), f32),
            kept(weight.shape, bf16),
            kept(weight.shape, bf16),
            kept((pairs, block * width), f32),
            kept((right_count, left_all, pair_width), f32),
            kept((n, right_count, left_count, pair_width), f32),
            kept((right_lanes // LANES, left_all * width, LANES), f32),
            kept((n, share, left_lanes), f32),
            kept((n, share, left_lanes), f32),
            kept((2, half, pair_width), f32),
            kept((half, pair_width), f32),
            kept((2, half, pair_width), f32),
            kept((half, pair_width), f32),
            kept((half, pair_width), f32),
            kept((2, half, pair_width), f32),
            dma((5,)),
            dma((n,)), dma((n,)), dma((n,)), dma((n,)),
            dma((n,)), dma((n,)), dma((n,)), dma((n,)),
            dma((n,)), dma((n,)), dma((n,)), dma((n,)),
            dma((n,)), dma((n,)), dma((5,)), dma((5,)),
        ],
        compiler_params=pltpu.CompilerParams(
            collective_id=0, has_side_effects=True, vmem_limit_bytes=40 * 2**20
        ),
    )(*(
        pltpu.with_memory_space_constraint(value, pltpu.HBM) for value in (
            left_act.reshape(share * left_count, width),
            right_act.reshape(share * right_count, width),
            weight,
            bias.reshape(1, pair_width),
            cotangent,
        )
    ))
    pair, gl, gr, gw = pl.pallas_call(
        write_kernel,
        out_shape=tuple(jax.ShapeDtypeStruct(s, f32) for s in shapes),
        in_specs=[vmem] * 4,
        out_specs=(hbm,) * 4,
        scratch_shapes=[dma((4,))],
    )(*(pltpu.with_memory_space_constraint(value, pltpu.VMEM) for value in results))
    return (
        pair.reshape(cotangent.shape),
        gl.reshape(left_act.shape),
        gr.reshape(right_act.shape),
        gw,
    )


def block_terms(left_block, right_full, cot_block, weight_cube, bias):
    seqs = right_full.shape[0]
    highest = lax.Precision.HIGHEST
    products = jnp.einsum("sic,sjd->icjd", left_block, right_full, precision=highest) / seqs
    pair_block = jnp.einsum("icjd,cdz->ijz", products, weight_cube, precision=highest) + bias
    grad_outer = jnp.einsum("ijz,cdz->icjd", cot_block, weight_cube, precision=highest)
    weight_term = jnp.einsum("icjd,ijz->cdz", products, cot_block, precision=highest)
    left_term = jnp.einsum("icjd,sjd->sic", grad_outer, right_full, precision=highest) / seqs
    right_term = jnp.einsum("icjd,sic->sjd", grad_outer, left_block, precision=highest) / seqs
    return (pair_block, weight_term, left_term, right_term)


def general(left_act, right_act, weight, bias, cotangent):
    width = left_act.shape[2]
    pair_width = weight.shape[1]
    widened = lax.all_gather(left_act, "col", axis=1, tiled=True)
    left_full = lax.all_to_all(widened, "row", split_axis=1, concat_axis=0, tiled=True)
    right_full = lax.all_gather(right_act, "row", axis=0, tiled=True)
    weight_cube = weight.reshape(width, width, pair_width)
    pair, grad_cube, left_partial, right_partial = block_terms(
        left_full, right_full, cotangent, weight_cube, bias
    )
    returned = lax.all_to_all(left_partial, "row", split_axis=0, concat_axis=1, tiled=True)
    grad_left = lax.psum_scatter(returned, "col", scatter_dimension=1, tiled=True)
    grad_right = lax.psum_scatter(right_partial, "row", scatter_dimension=0, tiled=True)
    grad_flat = grad_cube.reshape(width * width, pair_width)
    weight_part = lax.psum_scatter(grad_flat, "row", scatter_dimension=0, tiled=True)
    grad_weight = lax.psum(weight_part, "col")
    return (pair, grad_left, grad_right, grad_weight)


def shards(rows, cols, left_act, right_act, weight, bias, cotangent):
    share, right_count, width = right_act.shape
    left_count = cotangent.shape[0]
    fits = (
        rows == cols == 4
        and left_count == right_count == SUBLANES
        and share == width
        and share * rows == LANES
        and 4 * width == LANES
        and 4 * SUBLANES == width
        and weight.shape[1] == LANES
    )
    if fits:
        return fused(rows, left_act, right_act, weight, bias, cotangent)
    return general(left_act, right_act, weight, bias, cotangent)


def solution(mesh):
    placed = (
        P(("groups", "row"), "col", None),
        P(("groups", "row"), "col", None),
        P(),
        P(),
        P(("groups", "row"), "col", None),
    )
    return jax.shard_map(
        functools.partial(shards, mesh.shape["row"], mesh.shape["col"]),
        mesh=mesh,
        in_specs=placed,
        out_specs=(
            P(("groups", "row"), "col", None),
            P(("groups", "row"), "col", None),
            P(("groups", "row"), "col", None),
            P(("groups", "row"), None),
        ),
        check_vma=False,
    )
```
